32 devices in a mesh: grp: 2 (over y), kx: 4 (over z), ky: 2 (over x), ex: 2 (over core).
Axes of the slice: x: 2, y: 2, z: 4, core: 2. Of those that a mesh axis runs over, the one named last changes fastest.
Arguments:
- basis: bfloat16 [1024, 4, 4, 1024], P(None, 'kx', ('ky', 'ex')), may hold values from -6 to 6
- ritz: bfloat16 [1024, 192], P('kx'), may hold values from -0.1875 to 0.1875
- phonon_g: bfloat16 [6, 4, 4, 16384], P(None, 'kx', ('ky', 'ex')), may hold values from -6 to 6
- band_index: int32 [8], replicated, may hold values from 0 to 15, as said below
- qshift: int32 [6], P('grp'), parts along dimension 0, may hold values from 0 to 63, as said below
Outputs:
- coupling: float32 [12, 192, 192], P('grp', 'kx', ('ky', 'ex')), parts along dimension 0
The draws below stay inside these ranges and needn't reach their ends.
There are 2 independent parts, one for each index of `grp`. The reference program is written for one: setup_inputs(seed, part) draws one part's arguments, and reference() takes and returns one part's arrays. A program takes and returns all parts, laid end to end along the dimension named above; an argument that names none is the same for every part. Nothing has to cross between parts.
Inputs may be any that keep to these rules, and one draw needn't show every extreme that they name: `qshift`: component 0 lies in 1 to 3, component 1 in 0 to 63, component 2 in 1 to 3; the same for all k-points of a part; in the first part component 1 is 63. `band_index`: the first 4 entries are distinct and below 8, the last 4 entries are distinct and at least 8.
All inputs are finite; a program needn't handle non-finite values.
Results may differ from the reference program's by a relative error of at most 0.0049.
Values may be sent and summed in bfloat16 or wider, within the bound.
A program may use at most 64 MiB of HBM per device.

```python
import math
import jax
import jax.numpy as jnp
from jax import lax

NB = 1024
NX = 192
NV = 4
NC = 4
ALLB = 16
MODES = 6
NKY = 64
NKX = 4
NKZ = 4


def draw_qshift(key, part):
    key_list = jax.random.split(key, 3)
    along_first = jax.random.randint(key_list[0], (), 1, NKX)
    random_second = jax.random.randint(key_list[1], (), 0, NKY)
    along_second = jnp.where(part == 0, NKY - 1, random_second)
    along_third = jax.random.randint(key_list[2], (), 1, NKZ)
    return jnp.stack([along_first, along_second, along_third]).astype(jnp.int32)


def draw_band_index(key, part):
    key_list = jax.random.split(key, 2)
    half_bands = ALLB // 2
    valence = jax.random.permutation(key_list[0], half_bands)[:NV]
    conduction = half_bands + jax.random.permutation(key_list[1], half_bands)[:NC]
    return jnp.concatenate([valence, conduction]).astype(jnp.int32)


def block_scale(key, extent, pieces, smallest, high):
    factor_of, own = 1.0, jax.random.fold_in(key, 6)
    for axis_at, shards_of in pieces:
        draws = jnp.exp(jax.random.uniform(jax.random.fold_in(own, axis_at), (shards_of,), jnp.float32, smallest / len(pieces), high / len(pieces)))
        factor_of = factor_of * jnp.repeat(draws, extent[axis_at] // shards_of).reshape([-1 if axis == axis_at else 1 for axis in range(len(extent))])
    return factor_of


def gaussian(stream_key, dims, spread, bound, cuts=(), kind=jnp.bfloat16):
    drawn = jax.random.normal(stream_key, dims, jnp.float32) * spread
    if len(cuts) > 0:
        drawn = block_scale(stream_key, dims, cuts, -0.22, 0.18) * drawn
    return jnp.clip(drawn, min=-bound, max=bound).astype(kind)


def setup_inputs(seed: int = 0, part: int = 0) -> dict:
    arg_keys = jax.random.split(jax.random.key(seed), 6)
    part_splits = jax.random.split(jax.random.fold_in(arg_keys[5], part), 6)
    basis = gaussian(arg_keys[0], (NB, NKX, NKZ, NV * NC * NKY), 1.0, 6.0, ((1, 4), (2, 4)))
    ritz = gaussian(arg_keys[1], (NB, NX), NB ** -0.5, 0.1875, ((0, 4),))
    phonon_g = gaussian(arg_keys[2], (MODES, NKX, NKZ, ALLB * ALLB * NKY), 1.0, 6.0, ((1, 4), (2, 4)))
    band_index = draw_band_index(jax.random.fold_in(arg_keys[5], 71), part)
    qshift = draw_qshift(jax.random.fold_in(jax.random.fold_in(arg_keys[5], part), 71), part)
    return {"basis": basis, "ritz": ritz, "phonon_g": phonon_g, "band_index": band_index, "qshift": qshift}


def band_mix(amplitude, cond_mode, val_mode):
    cond_part = lax.optimization_barrier(jnp.sum(cond_mode[None, None] * amplitude[:, :, None], axis=3))
    val_part = lax.optimization_barrier(jnp.sum(val_mode[None, :, :, None] * amplitude[:, :, None], axis=1))
    return cond_part - val_part

def reference(basis, ritz, phonon_g, band_index, qshift):
    ritz_wide = ritz.astype(jnp.float32).T

    def rotate_plane(plane_index):
        plane_basis = lax.dynamic_index_in_dim(basis, plane_index, 1, keepdims=False)
        plane_basis = plane_basis.reshape(NB, NKZ, NV, NC, NKY).transpose(0, 2, 3, 1, 4)
        basis_flat = plane_basis.reshape(NB, -1).astype(jnp.float32)
        product = jnp.dot(ritz_wide, basis_flat, precision=lax.Precision.HIGHEST)
        return product.astype(jnp.bfloat16).reshape(NX, NV, NC, NKZ * NKY)
    excitons = lax.map(rotate_plane, jnp.arange(NKX, dtype=jnp.int32))
    grid = excitons.reshape(NKX, NX, NV, NC, NKZ, NKY)
    shifted = jnp.roll(grid, -qshift[0], axis=0)
    shifted = jnp.roll(shifted, -qshift[2], axis=4)
    shifted = jnp.roll(shifted, -qshift[1], axis=5)
    shifted = shifted.reshape(NKX, NX, NV * NC * NKZ * NKY)
    coupling_table = phonon_g.astype(jnp.float32).reshape(MODES, NKX, NKZ, ALLB, ALLB, NKY)
    coupling_table = coupling_table.transpose(0, 3, 4, 1, 2, 5)
    val_index = band_index[:NV]
    cond_index = band_index[NV:]
    val_table = coupling_table[:, val_index][:, :, val_index].reshape(MODES, NV, NV, NKX, NKZ * NKY)
    cond_table = coupling_table[:, cond_index][:, :, cond_index].reshape(MODES, NC, NC, NKX, NKZ * NKY)

    def add_plane(running, plane_index):
        amplitude = excitons[plane_index].astype(jnp.float32)
        shifted_rows = shifted[plane_index].astype(jnp.float32)
        terms = []
        for mode_index in range(MODES):
            cond_mode = cond_table[mode_index, :, :, plane_index]
            val_mode = val_table[mode_index, :, :, plane_index]
            mixed_band = band_mix(amplitude, cond_mode, val_mode).astype(jnp.bfloat16)
            mixed_band = lax.optimization_barrier(mixed_band).astype(jnp.float32)
            terms.append(jnp.dot(shifted_rows, mixed_band.reshape(NX, -1).T, precision=lax.Precision.HIGHEST))
        return (running + jnp.stack(terms), None)
    start_sum = jnp.zeros((MODES, NX, NX), jnp.float32)
    running, unused = lax.scan(add_plane, start_sum, jnp.arange(NKX, dtype=jnp.int32))
    return running * (1.0 / math.sqrt(NV * NC * NKX * NKY * NKZ))
```

```python
import functools
import math

import jax
import jax.numpy as jnp
from jax import lax
from jax.experimental import pallas as pl
from jax.experimental.pallas import tpu as pltpu
from jax.sharding import PartitionSpec as P

NV = 4
NC = 4
ALLB = 16
LANES = 128
MESH = pl.DeviceIdType.MESH


def passed_along(value, axis, steps):
    count = lax.axis_size(axis)
    pairs = [(source, (source + steps) % count) for source in range(count)]
    return lax.ppermute(value, axis, pairs)


def band_mix(amplitude, cond_mode, val_mode):
    cond_part = jnp.sum(cond_mode[None, None] * amplitude[:, :, None], axis=3)
    val_part = jnp.sum(val_mode[None, :, :, None] * amplitude[:, :, None], axis=1)
    return cond_part - val_part


def band_tables(phonon_g, band_index, count_val):
    all_bands = ALLB
    labels = jnp.arange(all_bands, dtype=jnp.int32)
    selector = (band_index[:, None] == labels[None, :]).astype(jnp.bfloat16)
    val_select = selector[:count_val]
    cond_select = selector[count_val:]
    coupling_table = phonon_g.reshape(phonon_g.shape[0], all_bands, all_bands, -1)
    val_table = jnp.einsum(
        "ia,uabk,jb->uijk",
        val_select,
        coupling_table,
        val_select,
        preferred_element_type=jnp.float32,
    )
    cond_table = jnp.einsum(
        "ia,uabk,jb->uijk",
        cond_select,
        coupling_table,
        cond_select,
        preferred_element_type=jnp.float32,
    )
    return (val_table, cond_table)


def by_collectives(basis, ritz, phonon_g, band_index, qshift):
    count_exc = ritz.shape[1]
    count_val = NV
    count_cond = NC
    width_y = basis.shape[3] // (count_val * count_cond)
    basis_flat = basis.reshape(basis.shape[0], -1)
    excitons = lax.dot_general(
        lax.all_gather(ritz, "kx", axis=0, tiled=True),
        basis_flat,
        (((0,), (0,)), ((), ())),
        preferred_element_type=jnp.float32,
    ).astype(jnp.bfloat16)
    planes_x = lax.axis_size("kx")
    planes_z = lax.axis_size(("ky", "ex"))
    carried = excitons
    for bit_place in range(planes_x.bit_length() - 1):
        arrived = passed_along(carried, "kx", -(1 << bit_place))
        carried = jnp.where(qshift[0] // (1 << bit_place) % 2 == 1, arrived, carried)
    for bit_place in range(planes_z.bit_length() - 1):
        arrived = passed_along(carried, ("ky", "ex"), -(1 << bit_place))
        carried = jnp.where(qshift[2] // (1 << bit_place) % 2 == 1, arrived, carried)
    shifted = jnp.roll(
        carried.reshape(count_exc, count_val, count_cond, width_y), -qshift[1], axis=3
    )
    shifted_rows = shifted.reshape(count_exc, -1)
    amplitude = excitons.reshape(count_exc, count_val, count_cond, width_y).astype(jnp.float32)
    val_table, cond_table = band_tables(phonon_g, band_index, count_val)
    blocks = []
    for mode_index in range(phonon_g.shape[0]):
        mixed_band = band_mix(amplitude, cond_table[mode_index], val_table[mode_index]).astype(
            jnp.bfloat16
        )
        blocks.append(
            lax.dot_general(
                shifted_rows,
                mixed_band.reshape(count_exc, -1),
                (((1,), (1,)), ((), ())),
                preferred_element_type=jnp.float32,
            )
        )
    partial_value = jnp.stack(blocks)
    norm_factor = 1.0 / math.sqrt(count_val * count_cond * width_y * planes_x * planes_z)
    own_cols = lax.psum_scatter(partial_value, ("ky", "ex"), scatter_dimension=2, tiled=True)
    coupling = lax.psum_scatter(own_cols, "kx", scatter_dimension=1, tiled=True)
    return coupling * norm_factor


def tables(planes_x, planes_z, band_ref, q_ref, phonon_ref, coefs, permute, wanted):
    modes = phonon_ref.shape[0]
    halves = NC // 2
    lane = lax.broadcasted_iota(jnp.int32, (modes, LANES), 1)
    low = lane < LANES // 2

    def on_both(left, right):
        row = band_ref[left] * ALLB + band_ref[right]
        at = pl.multiple_of((row // 2) * LANES, LANES)
        tile = phonon_ref[:, pl.ds(at, LANES)].astype(jnp.float32)
        other = pltpu.roll(tile, LANES // 2, 1)
        odd = row % 2
        return jnp.where(low == (odd == 0), tile, other)

    for w in range(NV):
        for v in range(NV):
            coefs[w * NV + v, :modes, :] = on_both(w, v)
    for ch in range(halves):
        for dh in range(halves):
            for off in range(2):
                lower = on_both(NV + 2 * ch, NV + 2 * dh + off)
                upper = on_both(NV + 2 * ch + 1, NV + 2 * dh + 1 - off)
                place = NV * NV + (ch * halves + dh) * 2 + off
                coefs[place, :modes, :] = jnp.where(low, lower, upper)

    come = lax.broadcasted_iota(jnp.int32, (LANES, LANES), 0)
    goes = lax.broadcasted_iota(jnp.int32, (LANES, LANES), 1)
    width = LANES // 2
    source = (goes // width) * width + (goes % width + q_ref[1]) % width
    permute[...] = (come == source).astype(jnp.bfloat16)

    for target in range(planes_x * planes_z):
        x = (target // planes_z + q_ref[0]) % planes_x
        z = (target % planes_z + q_ref[2]) % planes_z
        wanted[target : target + 1, :] = jnp.full((1, LANES), x * planes_z + z, jnp.int32)


def whole_step(
    planes_x, planes_z, norm_factor,
    coefs, permute, wanted, ritz_ref, basis_ref, out_ref,
    gathered, total, exc_ref, slices, first, second_out, second_in,
    mixed, shifted, sum_out, sum_in, turned, last_out, last_in,
    ritz_send, ritz_recv, fwd_send, fwd_recv,
    one_send, one_recv, two_send, two_recv, a_send, a_recv, b_send, b_recv,
):
    planes = planes_x * planes_z
    grp = lax.axis_index("grp")
    kx = lax.axis_index("kx")
    ky = lax.axis_index("ky")
    ex = lax.axis_index("ex")
    kz = ky * 2 + ex
    me = kx * planes_z + kz
    modes = out_ref.shape[0]
    count_exc, depth = ritz_ref.shape
    half = depth // 2
    tiles = exc_ref.shape[1] // LANES
    halves = NC // 2

    def device(plane):
        z = plane % planes_z
        return (grp, plane // planes_z, z // 2, z % 2)

    barrier = pltpu.get_barrier_semaphore()
    for step in range(1, planes):
        pl.semaphore_signal(
            barrier, inc=1, device_id=device((me + step) % planes), device_id_type=MESH
        )
    gathered[kx, 0] = ritz_ref[:, :half]
    gathered[kx, 1] = ritz_ref[:, half:]

    pl.semaphore_wait(barrier, planes - 1)

    asks = []
    for step in range(1, planes_x):
        ask = pltpu.make_async_remote_copy(
            src_ref=gathered.at[kx, ex],
            dst_ref=gathered.at[kx, ex],
            send_sem=ritz_send.at[step - 1],
            recv_sem=ritz_recv.at[step - 1],
            device_id=(grp, (kx + step) % planes_x, ky, ex),
            device_id_type=MESH,
        )
        ask.start()
        asks.append(ask)

    def rotate(source):
        rows = jnp.concatenate([gathered[source, 0], gathered[source, 1]], axis=1)
        at = pl.multiple_of(source * depth, depth)
        return jnp.dot(
            rows, basis_ref[pl.ds(at, depth), :], preferred_element_type=jnp.float32
        )

    total[...] = rotate(kx)
    hands = []
    for step in range(1, planes_x):
        asks[step - 1].wait_recv()
        source = (kx - step + planes_x) % planes_x
        hand = pltpu.make_async_remote_copy(
            src_ref=gathered.at[source, ex],
            dst_ref=gathered.at[source, ex],
            send_sem=fwd_send.at[step - 1],
            recv_sem=fwd_recv.at[step - 1],
            device_id=(grp, kx, ky, 1 - ex),
            device_id_type=MESH,
        )
        hand.start()
        hands.append(hand)
    for step in range(1, planes_x):
        hands[step - 1].wait_recv()
        source = (kx - step + planes_x) % planes_x
        total[...] += rotate(source)
    exc_ref[...] = total[...].astype(jnp.bfloat16)

    cuts = planes // tiles
    rows_cut = count_exc // cuts
    for tile in range(tiles):
        moved = jnp.dot(
            exc_ref[:, tile * LANES : (tile + 1) * LANES],
            permute[...],
            preferred_element_type=jnp.float32,
        ).astype(jnp.bfloat16)
        for cut in range(cuts):
            slices[cut * tiles + tile] = moved[cut * rows_cut : (cut + 1) * rows_cut]

    ones = []
    for step in range(1, planes):
        target = (me + step) % planes
        one = pltpu.make_async_remote_copy(
            src_ref=slices.at[target],
            dst_ref=first.at[me],
            send_sem=one_send.at[step - 1],
            recv_sem=one_recv.at[step - 1],
            device_id=device(target),
            device_id_type=MESH,
        )
        one.start()
        ones.append(one)
    first[me] = slices[me]

    own_rows = count_exc // planes_z
    chunk = 16
    per_block = own_rows // chunk

    def mix_rows(index, carry):
        at = pl.multiple_of(index * chunk, chunk)
        straight = []
        crossed = []
        for tile in range(tiles):
            part = exc_ref[pl.ds(at, chunk), tile * LANES : (tile + 1) * LANES].astype(jnp.float32)
            straight.append(part)
            crossed.append(pltpu.roll(part, LANES // 2, 1))
        block = index // per_block
        row = pl.multiple_of((index % per_block) * chunk, chunk)

        def mix_mode(u, inner):
            for v in range(NV):
                for ch in range(halves):
                    value = None
                    for dh in range(halves):
                        for off in range(2):
                            factor = coefs[NV * NV + (ch * halves + dh) * 2 + off, pl.ds(u, 1), :]
                            term = factor * (crossed if off else straight)[v * halves + dh]
                            value = term if value is None else value + term
                    minus = None
                    for w in range(NV):
                        term = coefs[w * NV + v, pl.ds(u, 1), :] * straight[w * halves + ch]
                        minus = term if minus is None else minus + term
                    tile = v * halves + ch
                    mixed[block, u, pl.ds(row, chunk), tile * LANES : (tile + 1) * LANES] = (
                        value - minus
                    ).astype(jnp.bfloat16)
            return inner

        return lax.fori_loop(0, modes, mix_mode, carry)

    lax.fori_loop(0, count_exc // chunk, mix_rows, 0)

    for one in ones:
        one.wait_recv()

    def pick(target):
        plane = wanted[pl.ds(target, 1), :]
        value = first[0]
        for other in range(1, planes):
            value = jnp.where(plane == other, first[other], value)
        return value

    twos = []
    for step in range(1, planes):
        target = (me + step) % planes
        second_out[target] = pick(target)
        two = pltpu.make_async_remote_copy(
            src_ref=second_out.at[target],
            dst_ref=second_in.at[me],
            send_sem=two_send.at[step - 1],
            recv_sem=two_recv.at[step - 1],
            device_id=device(target),
            device_id_type=MESH,
        )
        two.start()
        twos.append(two)
    second_in[me] = pick(me)
    for two in twos:
        two.wait_recv()
    for cut in range(cuts):
        for tile in range(tiles):
            shifted[cut * rows_cut : (cut + 1) * rows_cut, tile * LANES : (tile + 1) * LANES] = (
                second_in[cut * tiles + tile]
            )

    def product(block):
        left = mixed[block].reshape(modes * own_rows, tiles * LANES)
        return lax.dot_general(
            left, shifted[...], (((1,), (1,)), ((), ())), preferred_element_type=jnp.float32
        )

    sums = []
    for step in range(1, planes_z):
        block = (kz + step) % planes_z
        sum_out[step - 1] = product(block).astype(jnp.bfloat16)
        one_sum = pltpu.make_async_remote_copy(
            src_ref=sum_out.at[step - 1],
            dst_ref=sum_in.at[step - 1],
            send_sem=a_send.at[step - 1],
            recv_sem=a_recv.at[step - 1],
            device_id=(grp, kx, block // 2, block % 2),
            device_id_type=MESH,
        )
        one_sum.start()
        sums.append(one_sum)
    mine = product(kz)
    for step in range(1, planes_z):
        sums[step - 1].wait_recv()
        mine = mine + sum_in[step - 1].astype(jnp.float32)
    flipped = mine.T
    out_rows = count_exc // planes_x
    for block in range(planes_x):
        turned[block] = flipped[block * out_rows : (block + 1) * out_rows]
    lasts = []
    for step in range(1, planes_x):
        block = (kx + step) % planes_x
        last_out[step - 1] = turned[block].astype(jnp.bfloat16)
        one_last = pltpu.make_async_remote_copy(
            src_ref=last_out.at[step - 1],
            dst_ref=last_in.at[step - 1],
            send_sem=b_send.at[step - 1],
            recv_sem=b_recv.at[step - 1],
            device_id=(grp, block, ky, ex),
            device_id_type=MESH,
        )
        one_last.start()
        lasts.append(one_last)
    result = turned[kx]
    for step in range(1, planes_x):
        lasts[step - 1].wait_recv()
        result = result + last_in[step - 1].astype(jnp.float32)
    result = result * norm_factor
    for u in range(modes):
        out_ref[u] = result[:, u * own_rows : (u + 1) * own_rows]
    for started in asks + hands + ones + twos + sums + lasts:
        started.wait_send()


def by_kernel(basis, ritz, phonon_g, band_index, qshift):
    planes_x = lax.axis_size("kx")
    planes_z = lax.axis_size(("ky", "ex"))
    planes = planes_x * planes_z
    count_basis, count_trans = basis.shape[0], basis.shape[3]
    depth, count_exc = ritz.shape
    modes = phonon_g.shape[0]
    tiles = count_trans // LANES
    rows_cut = count_exc // (planes // tiles)
    own = count_exc // planes_z
    out_rows = count_exc // planes_x
    norm_factor = 1.0 / math.sqrt(count_trans * planes)
    bf16 = jnp.bfloat16
    dma = pltpu.SemaphoreType.DMA
    vmem = pl.BlockSpec(memory_space=pltpu.VMEM)
    smem = pl.BlockSpec(memory_space=pltpu.SMEM)
    coefs, permute, wanted = pl.pallas_call(
        functools.partial(tables, planes_x, planes_z),
        out_shape=(
            jax.ShapeDtypeStruct((NV * NV + NC * NC // 2, 8, LANES), jnp.float32),
            jax.ShapeDtypeStruct((LANES, LANES), bf16),
            jax.ShapeDtypeStruct((planes, LANES), jnp.int32),
        ),
        in_specs=[smem, smem, vmem],
        out_specs=(vmem, vmem, vmem),
    )(band_index, qshift, phonon_g.reshape(modes, -1))
    return pl.pallas_call(
        functools.partial(whole_step, planes_x, planes_z, norm_factor),
        out_shape=jax.ShapeDtypeStruct((modes, out_rows, own), jnp.float32),
        in_specs=[vmem] * 5,
        out_specs=vmem,
        scratch_shapes=[
            pltpu.VMEM((planes_x, 2, count_exc, depth // 2), bf16),
            pltpu.VMEM((count_exc, count_trans), jnp.float32),
            pltpu.VMEM((count_exc, count_trans), bf16),
            pltpu.VMEM((planes, rows_cut, LANES), bf16),
            pltpu.VMEM((planes, rows_cut, LANES), bf16),
            pltpu.VMEM((planes, rows_cut, LANES), bf16),
            pltpu.VMEM((planes, rows_cut, LANES), bf16),
            pltpu.VMEM((planes_z, modes, own, count_trans), bf16),
            pltpu.VMEM((count_exc, count_trans), bf16),
            pltpu.VMEM((planes_z - 1, modes * own, count_exc), bf16),
            pltpu.VMEM((planes_z - 1, modes * own, count_exc), bf16),
            pltpu.VMEM((planes_x, out_rows, modes * own), jnp.float32),
            pltpu.VMEM((planes_x - 1, out_rows, modes * own), bf16),
            pltpu.VMEM((planes_x - 1, out_rows, modes * own), bf16),
            dma((planes_x - 1,)),
            dma((planes_x - 1,)),
            dma((planes_x - 1,)),
            dma((planes_x - 1,)),
            dma((planes - 1,)),
            dma((planes - 1,)),
            dma((planes - 1,)),
            dma((planes - 1,)),
            dma((planes_z - 1,)),
            dma((planes_z - 1,)),
            dma((planes_x - 1,)),
            dma((planes_x - 1,)),
        ],
        compiler_params=pltpu.CompilerParams(
            collective_id=0, has_side_effects=True, vmem_limit_bytes=40 << 20
        ),
    )(
        coefs,
        permute,
        wanted,
        ritz.T,
        basis.reshape(count_basis, count_trans),
    )


def shards(basis, ritz, phonon_g, band_index, qshift):
    planes_x = lax.axis_size("kx")
    planes_z = lax.axis_size(("ky", "ex"))
    planes = planes_x * planes_z
    count_exc = ritz.shape[1]
    tiles = basis.shape[3] // LANES
    whole_tiles = (
        basis.shape[3] == NV * NC * LANES // 2
        and lax.axis_size("ex") == 2
        and planes % tiles == 0
        and count_exc % (planes // tiles * 16) == 0
        and count_exc % (planes_z * 16) == 0
        and count_exc % (planes_x * 16) == 0
        and ritz.shape[0] % (2 * LANES) == 0
        and phonon_g.shape[0] <= 8
    )
    step = by_kernel if whole_tiles else by_collectives
    return step(basis, ritz, phonon_g, band_index, qshift)


def solution(mesh):
    placed = (
        P(None, "kx", ("ky", "ex"), None),
        P("kx", None),
        P(None, "kx", ("ky", "ex"), None),
        P(),
        P("grp"),
    )
    return jax.shard_map(
        shards, mesh=mesh, in_specs=placed, out_specs=P("grp", "kx", ("ky", "ex")), check_vma=False
    )
```

```python
import functools
import math

import jax
import jax.numpy as jnp
from jax import lax
from jax.experimental import pallas as pl
from jax.experimental.pallas import tpu as pltpu
from jax.sharding import PartitionSpec as P

NV = 4
NC = 4
ALLB = 16
LANES = 128
MESH = pl.DeviceIdType.MESH


def passed_along(value, axis, steps):
    count = lax.axis_size(axis)
    pairs = [(source, (source + steps) % count) for source in range(count)]
    return lax.ppermute(value, axis, pairs)


def band_mix(amplitude, cond_mode, val_mode):
    cond_part = jnp.sum(cond_mode[None, None] * amplitude[:, :, None], axis=3)
    val_part = jnp.sum(val_mode[None, :, :, None] * amplitude[:, :, None], axis=1)
    return cond_part - val_part


def band_tables(phonon_g, band_index, count_val):
    all_bands = ALLB
    labels = jnp.arange(all_bands, dtype=jnp.int32)
    selector = (band_index[:, None] == labels[None, :]).astype(jnp.bfloat16)
    val_select = selector[:count_val]
    cond_select = selector[count_val:]
    coupling_table = phonon_g.reshape(phonon_g.shape[0], all_bands, all_bands, -1)
    val_table = jnp.einsum(
        "ia,uabk,jb->uijk",
        val_select,
        coupling_table,
        val_select,
        preferred_element_type=jnp.float32,
    )
    cond_table = jnp.einsum(
        "ia,uabk,jb->uijk",
        cond_select,
        coupling_table,
        cond_select,
        preferred_element_type=jnp.float32,
    )
    return (val_table, cond_table)


def by_collectives(basis, ritz, phonon_g, band_index, qshift):
    count_exc = ritz.shape[1]
    count_val = NV
    count_cond = NC
    width_y = basis.shape[3] // (count_val * count_cond)
    basis_flat = basis.reshape(basis.shape[0], -1)
    excitons = lax.dot_general(
        lax.all_gather(ritz, "kx", axis=0, tiled=True),
        basis_flat,
        (((0,), (0,)), ((), ())),
        preferred_element_type=jnp.float32,
    ).astype(jnp.bfloat16)
    planes_x = lax.axis_size("kx")
    planes_z = lax.axis_size(("ky", "ex"))
    carried = excitons
    for bit_place in range(planes_x.bit_length() - 1):
        arrived = passed_along(carried, "kx", -(1 << bit_place))
        carried = jnp.where(qshift[0] // (1 << bit_place) % 2 == 1, arrived, carried)
    for bit_place in range(planes_z.bit_length() - 1):
        arrived = passed_along(carried, ("ky", "ex"), -(1 << bit_place))
        carried = jnp.where(qshift[2] // (1 << bit_place) % 2 == 1, arrived, carried)
    shifted = jnp.roll(
        carried.reshape(count_exc, count_val, count_cond, width_y), -qshift[1], axis=3
    )
    shifted_rows = shifted.reshape(count_exc, -1)
    amplitude = excitons.reshape(count_exc, count_val, count_cond, width_y).astype(jnp.float32)
    val_table, cond_table = band_tables(phonon_g, band_index, count_val)
    blocks = []
    for mode_index in range(phonon_g.shape[0]):
        mixed_band = band_mix(amplitude, cond_table[mode_index], val_table[mode_index]).astype(
            jnp.bfloat16
        )
        blocks.append(
            lax.dot_general(
                shifted_rows,
                mixed_band.reshape(count_exc, -1),
                (((1,), (1,)), ((), ())),
                preferred_element_type=jnp.float32,
            )
        )
    partial_value = jnp.stack(blocks)
    norm_factor = 1.0 / math.sqrt(count_val * count_cond * width_y * planes_x * planes_z)
    own_cols = lax.psum_scatter(partial_value, ("ky", "ex"), scatter_dimension=2, tiled=True)
    coupling = lax.psum_scatter(own_cols, "kx", scatter_dimension=1, tiled=True)
    return coupling * norm_factor


def whole_step(
    planes_x, planes_z, norm_factor,
    band_hbm, q_hbm, ritz_hbm, phonon_hbm, basis_hbm, out_ref,
    band_ref, q_ref, ritz_ref, phonon_ref, basis_ref, coefs, gathered, total, exc_ref, slices, first, second_out, second_in,
    mixed, shifted, sum_out, sum_in, turned, last_out, last_in,
    load_sems, ritz_send, ritz_recv, fwd_send, fwd_recv,
    one_send, one_recv, two_send, two_recv, a_send, a_recv, b_send, b_recv,
):
    planes = planes_x * planes_z
    grp = lax.axis_index("grp")
    kx = lax.axis_index("kx")
    ky = lax.axis_index("ky")
    ex = lax.axis_index("ex")
    kz = ky * 2 + ex
    me = kx * planes_z + kz
    modes = out_ref.shape[0]
    count_exc, depth = ritz_ref.shape
    half = depth // 2
    tiles = exc_ref.shape[1] // LANES
    halves = NC // 2

    def device(plane):
        z = plane % planes_z
        return (grp, plane // planes_z, z // 2, z % 2)

    barrier = pltpu.get_barrier_semaphore()
    for step in range(1, planes):
        pl.semaphore_signal(
            barrier, inc=1, device_id=device((me + step) % planes), device_id_type=MESH
        )
    loads = [
        pltpu.make_async_copy(source, place, load_sems.at[at])
        for at, (source, place) in enumerate(
            (
                (ritz_hbm, ritz_ref),
                (band_hbm, band_ref),
                (q_hbm, q_ref),
                (phonon_hbm, phonon_ref),
                (basis_hbm, basis_ref),
            )
        )
    ]
    for load in loads:
        load.start()
    loads[0].wait()
    gathered[kx, 0] = ritz_ref[:, :half]
    gathered[kx, 1] = ritz_ref[:, half:]
    pl.semaphore_wait(barrier, planes - 1)

    asks = []
    for step in range(1, planes_x):
        ask = pltpu.make_async_remote_copy(
            src_ref=gathered.at[kx, ex],
            dst_ref=gathered.at[kx, ex],
            send_sem=ritz_send.at[step - 1],
            recv_sem=ritz_recv.at[step - 1],
            device_id=(grp, (kx + step) % planes_x, ky, ex),
            device_id_type=MESH,
        )
        ask.start()
        asks.append(ask)

    for load in loads[1:4]:
        load.wait()
    lane = lax.broadcasted_iota(jnp.int32, (modes, LANES), 1)
    low = lane < LANES // 2
    bands = [jnp.full((modes, LANES), band_ref[slot], jnp.int32) for slot in range(NV + NC)]
    part = ALLB // 2
    row_tiles = part // 2

    def rows_of(slot, base):
        found = []
        for at in range(row_tiles):
            value = None
            for band in range(base, base + part):
                start = (band * part + base // 2 + at) * LANES
                tile = phonon_ref[:, start : start + LANES].astype(jnp.float32)
                value = tile if value is None else jnp.where(bands[slot] == band, tile, value)
            found.append(value)
        return found

    def on_both(found, slot, base):
        value = found[0]
        for at in range(1, row_tiles):
            value = jnp.where((bands[slot] >> 1) == base // 2 + at, found[at], value)
        other = pltpu.roll(value, LANES // 2, 1)
        upper = (bands[slot] & 1) == jnp.where(low, 0, 1)
        return jnp.where(upper, value, other)

    for w in range(NV):
        found = rows_of(w, 0)
        for v in range(NV):
            coefs[w * NV + v, :modes, :] = on_both(found, v, 0)
    for ch in range(halves):
        lower_rows = rows_of(NV + 2 * ch, part)
        upper_rows = rows_of(NV + 2 * ch + 1, part)
        for dh in range(halves):
            for off in range(2):
                lower = on_both(lower_rows, NV + 2 * dh + off, part)
                upper = on_both(upper_rows, NV + 2 * dh + 1 - off, part)
                place = NV * NV + (ch * halves + dh) * 2 + off
                coefs[place, :modes, :] = jnp.where(low, lower, upper)
    come = lax.broadcasted_iota(jnp.int32, (LANES, LANES), 0)
    goes = lax.broadcasted_iota(jnp.int32, (LANES, LANES), 1)
    width = LANES // 2
    along = jnp.full((LANES, LANES), q_ref[1], jnp.int32)
    permute = (come == (goes & width) + ((goes + along) & (width - 1))).astype(jnp.bfloat16)
    loads[4].wait()

    def rotate(source):
        rows = jnp.concatenate([gathered[source, 0], gathered[source, 1]], axis=1)
        at = pl.multiple_of(source * depth, depth)
        return jnp.dot(
            rows, basis_ref[pl.ds(at, depth), :], preferred_element_type=jnp.float32
        )

    total[...] = rotate(kx)
    hands = []
    for step in range(1, planes_x):
        asks[step - 1].wait_recv()
        source = (kx - step + planes_x) % planes_x
        hand = pltpu.make_async_remote_copy(
            src_ref=gathered.at[source, ex],
            dst_ref=gathered.at[source, ex],
            send_sem=fwd_send.at[step - 1],
            recv_sem=fwd_recv.at[step - 1],
            device_id=(grp, kx, ky, 1 - ex),
            device_id_type=MESH,
        )
        hand.start()
        hands.append(hand)
    for step in range(1, planes_x):
        hands[step - 1].wait_recv()
        source = (kx - step + planes_x) % planes_x
        total[...] += rotate(source)
    exc_ref[...] = total[...].astype(jnp.bfloat16)

    cuts = planes // tiles
    rows_cut = count_exc // cuts
    for tile in range(tiles):
        moved = jnp.dot(
            exc_ref[:, tile * LANES : (tile + 1) * LANES],
            permute,
            preferred_element_type=jnp.float32,
        ).astype(jnp.bfloat16)
        for cut in range(cuts):
            slices[cut * tiles + tile] = moved[cut * rows_cut : (cut + 1) * rows_cut]

    ones = []
    for step in range(1, planes):
        target = (me + step) % planes
        one = pltpu.make_async_remote_copy(
            src_ref=slices.at[target],
            dst_ref=first.at[me],
            send_sem=one_send.at[step - 1],
            recv_sem=one_recv.at[step - 1],
            device_id=device(target),
            device_id_type=MESH,
        )
        one.start()
        ones.append(one)
    first[me] = slices[me]

    own_rows = count_exc // planes_z
    chunk = 16
    per_block = own_rows // chunk

    def mix_rows(index, carry):
        at = pl.multiple_of(index * chunk, chunk)
        straight = []
        crossed = []
        for tile in range(tiles):
            part = exc_ref[pl.ds(at, chunk), tile * LANES : (tile + 1) * LANES].astype(jnp.float32)
            straight.append(part)
            crossed.append(pltpu.roll(part, LANES // 2, 1))
        block = index // per_block
        row = pl.multiple_of((index % per_block) * chunk, chunk)

        def mix_mode(u, inner):
            for v in range(NV):
                for ch in range(halves):
                    value = None
                    for dh in range(halves):
                        for off in range(2):
                            factor = coefs[NV * NV + (ch * halves + dh) * 2 + off, pl.ds(u, 1), :]
                            term = factor * (crossed if off else straight)[v * halves + dh]
                            value = term if value is None else value + term
                    minus = None
                    for w in range(NV):
                        term = coefs[w * NV + v, pl.ds(u, 1), :] * straight[w * halves + ch]
                        minus = term if minus is None else minus + term
                    tile = v * halves + ch
                    mixed[block, u, pl.ds(row, chunk), tile * LANES : (tile + 1) * LANES] = (
                        value - minus
                    ).astype(jnp.bfloat16)
            return inner

        return lax.fori_loop(0, modes, mix_mode, carry)

    lax.fori_loop(0, count_exc // chunk, mix_rows, 0)

    for one in ones:
        one.wait_recv()

    along_x = jnp.full((1, LANES), q_ref[0], jnp.int32)
    along_z = jnp.full((1, LANES), q_ref[2], jnp.int32)

    def pick(target):
        x, z = target // planes_z, target % planes_z
        value = None
        for dx in range(1, planes_x):
            for dz in range(1, planes_z):
                plane = ((x + dx) % planes_x) * planes_z + (z + dz) % planes_z
                there = first[plane]
                if value is None:
                    value = there
                else:
                    value = jnp.where((along_x == dx) & (along_z == dz), there, value)
        return value

    twos = []
    for step in range(1, planes):
        target = (me + step) % planes
        second_out[target] = pick(target)
        two = pltpu.make_async_remote_copy(
            src_ref=second_out.at[target],
            dst_ref=second_in.at[me],
            send_sem=two_send.at[step - 1],
            recv_sem=two_recv.at[step - 1],
            device_id=device(target),
            device_id_type=MESH,
        )
        two.start()
        twos.append(two)
    second_in[me] = pick(me)
    for two in twos:
        two.wait_recv()
    for cut in range(cuts):
        for tile in range(tiles):
            shifted[cut * rows_cut : (cut + 1) * rows_cut, tile * LANES : (tile + 1) * LANES] = (
                second_in[cut * tiles + tile]
            )

    def product(block):
        left = mixed[block].reshape(modes * own_rows, tiles * LANES)
        return lax.dot_general(
            left, shifted[...], (((1,), (1,)), ((), ())), preferred_element_type=jnp.float32
        )

    sums = []
    for step in range(1, planes_z):
        block = (kz + step) % planes_z
        sum_out[step - 1] = product(block).astype(jnp.bfloat16)
        one_sum = pltpu.make_async_remote_copy(
            src_ref=sum_out.at[step - 1],
            dst_ref=sum_in.at[step - 1],
            send_sem=a_send.at[step - 1],
            recv_sem=a_recv.at[step - 1],
            device_id=(grp, kx, block // 2, block % 2),
            device_id_type=MESH,
        )
        one_sum.start()
        sums.append(one_sum)
    mine = product(kz)
    for step in range(1, planes_z):
        sums[step - 1].wait_recv()
        mine = mine + sum_in[step - 1].astype(jnp.float32)
    flipped = mine.T
    out_rows = count_exc // planes_x
    for block in range(planes_x):
        turned[block] = flipped[block * out_rows : (block + 1) * out_rows]
    lasts = []
    for step in range(1, planes_x):
        block = (kx + step) % planes_x
        last_out[step - 1] = turned[block].astype(jnp.bfloat16)
        one_last = pltpu.make_async_remote_copy(
            src_ref=last_out.at[step - 1],
            dst_ref=last_in.at[step - 1],
            send_sem=b_send.at[step - 1],
            recv_sem=b_recv.at[step - 1],
            device_id=(grp, block, ky, ex),
            device_id_type=MESH,
        )
        one_last.start()
        lasts.append(one_last)
    result = turned[kx]
    for step in range(1, planes_x):
        lasts[step - 1].wait_recv()
        result = result + last_in[step - 1].astype(jnp.float32)
    result = result * norm_factor
    for u in range(modes):
        out_ref[u] = result[:, u * own_rows : (u + 1) * own_rows]
    for started in asks + hands + ones + twos + sums + lasts:
        started.wait_send()


def by_kernel(basis, ritz, phonon_g, band_index, qshift):
    planes_x = lax.axis_size("kx")
    planes_z = lax.axis_size(("ky", "ex"))
    planes = planes_x * planes_z
    count_basis, count_trans = basis.shape[0], basis.shape[3]
    depth, count_exc = ritz.shape
    modes = phonon_g.shape[0]
    tiles = count_trans // LANES
    rows_cut = count_exc // (planes // tiles)
    own = count_exc // planes_z
    out_rows = count_exc // planes_x
    norm_factor = 1.0 / math.sqrt(count_trans * planes)
    bf16 = jnp.bfloat16
    dma = pltpu.SemaphoreType.DMA
    vmem = pl.BlockSpec(memory_space=pltpu.VMEM)
    stay = pl.BlockSpec(memory_space=pl.ANY)
    return pl.pallas_call(
        functools.partial(whole_step, planes_x, planes_z, norm_factor),
        out_shape=jax.ShapeDtypeStruct((modes, out_rows, own), jnp.float32),
        in_specs=[stay] * 5,
        out_specs=vmem,
        scratch_shapes=[
            pltpu.SMEM(band_index.shape, jnp.int32),
            pltpu.SMEM(qshift.shape, jnp.int32),
            pltpu.VMEM((count_exc, depth), bf16),
            pltpu.VMEM((modes, phonon_g.shape[3]), bf16),
            pltpu.VMEM((count_basis, count_trans), bf16),
            pltpu.VMEM((NV * NV + NC * NC // 2, 8, LANES), jnp.float32),
            pltpu.VMEM((planes_x, 2, count_exc, depth // 2), bf16),
            pltpu.VMEM((count_exc, count_trans), jnp.float32),
            pltpu.VMEM((count_exc, count_trans), bf16),
            pltpu.VMEM((planes, rows_cut, LANES), bf16),
            pltpu.VMEM((planes, rows_cut, LANES), bf16),
            pltpu.VMEM((planes, rows_cut, LANES), bf16),
            pltpu.VMEM((planes, rows_cut, LANES), bf16),
            pltpu.VMEM((planes_z, modes, own, count_trans), bf16),
            pltpu.VMEM((count_exc, count_trans), bf16),
            pltpu.VMEM((planes_z - 1, modes * own, count_exc), bf16),
            pltpu.VMEM((planes_z - 1, modes * own, count_exc), bf16),
            pltpu.VMEM((planes_x, out_rows, modes * own), jnp.float32),
            pltpu.VMEM((planes_x - 1, out_rows, modes * own), bf16),
            pltpu.VMEM((planes_x - 1, out_rows, modes * own), bf16),
            dma((5,)),
            dma((planes_x - 1,)),
            dma((planes_x - 1,)),
            dma((planes_x - 1,)),
            dma((planes_x - 1,)),
            dma((planes - 1,)),
            dma((planes - 1,)),
            dma((planes - 1,)),
            dma((planes - 1,)),
            dma((planes_z - 1,)),
            dma((planes_z - 1,)),
            dma((planes_x - 1,)),
            dma((planes_x - 1,)),
        ],
        compiler_params=pltpu.CompilerParams(
            collective_id=0, has_side_effects=True, vmem_limit_bytes=60 << 20
        ),
    )(
        band_index,
        qshift,
        ritz.T,
        phonon_g.reshape(modes, -1),
        basis.reshape(count_basis, count_trans),
    )


def shards(basis, ritz, phonon_g, band_index, qshift):
    planes_x = lax.axis_size("kx")
    planes_z = lax.axis_size(("ky", "ex"))
    planes = planes_x * planes_z
    count_exc = ritz.shape[1]
    tiles = basis.shape[3] // LANES
    whole_tiles = (
        basis.shape[3] == NV * NC * LANES // 2
        and lax.axis_size("ex") == 2
        and planes % tiles == 0
        and count_exc % (planes // tiles * 16) == 0
        and count_exc % (planes_z * 16) == 0
        and count_exc % (planes_x * 16) == 0
        and ritz.shape[0] % (2 * LANES) == 0
        and phonon_g.shape[0] <= 8
    )
    step = by_kernel if whole_tiles else by_collectives
    return step(basis, ritz, phonon_g, band_index, qshift)


def solution(mesh):
    placed = (
        P(None, "kx", ("ky", "ex"), None),
        P("kx", None),
        P(None, "kx", ("ky", "ex"), None),
        P(),
        P("grp"),
    )
    return jax.shard_map(
        shards, mesh=mesh, in_specs=placed, out_specs=P("grp", "kx", ("ky", "ex")), check_vma=False
    )
```

```python
import functools
import math

import jax
import jax.numpy as jnp
from jax import lax
from jax.experimental import pallas as pl
from jax.experimental.pallas import tpu as pltpu
from jax.sharding import PartitionSpec as P

NV = 4
NC = 4
ALLB = 16
LANES = 128
MESH = pl.DeviceIdType.MESH


def passed_along(value, axis, steps):
    count = lax.axis_size(axis)
    pairs = [(source, (source + steps) % count) for source in range(count)]
    return lax.ppermute(value, axis, pairs)


def band_mix(amplitude, cond_mode, val_mode):
    cond_part = jnp.sum(cond_mode[None, None] * amplitude[:, :, None], axis=3)
    val_part = jnp.sum(val_mode[None, :, :, None] * amplitude[:, :, None], axis=1)
    return cond_part - val_part


def band_tables(phonon_g, band_index, count_val):
    all_bands = ALLB
    labels = jnp.arange(all_bands, dtype=jnp.int32)
    selector = (band_index[:, None] == labels[None, :]).astype(jnp.bfloat16)
    val_select = selector[:count_val]
    cond_select = selector[count_val:]
    coupling_table = phonon_g.reshape(phonon_g.shape[0], all_bands, all_bands, -1)
    val_table = jnp.einsum(
        "ia,uabk,jb->uijk",
        val_select,
        coupling_table,
        val_select,
        preferred_element_type=jnp.float32,
    )
    cond_table = jnp.einsum(
        "ia,uabk,jb->uijk",
        cond_select,
        coupling_table,
        cond_select,
        preferred_element_type=jnp.float32,
    )
    return (val_table, cond_table)


def by_collectives(basis, ritz, phonon_g, band_index, qshift):
    count_exc = ritz.shape[1]
    count_val = NV
    count_cond = NC
    width_y = basis.shape[3] // (count_val * count_cond)
    basis_flat = basis.reshape(basis.shape[0], -1)
    excitons = lax.dot_general(
        lax.all_gather(ritz, "kx", axis=0, tiled=True),
        basis_flat,
        (((0,), (0,)), ((), ())),
        preferred_element_type=jnp.float32,
    ).astype(jnp.bfloat16)
    planes_x = lax.axis_size("kx")
    planes_z = lax.axis_size(("ky", "ex"))
    carried = excitons
    for bit_place in range(planes_x.bit_length() - 1):
        arrived = passed_along(carried, "kx", -(1 << bit_place))
        carried = jnp.where(qshift[0] // (1 << bit_place) % 2 == 1, arrived, carried)
    for bit_place in range(planes_z.bit_length() - 1):
        arrived = passed_along(carried, ("ky", "ex"), -(1 << bit_place))
        carried = jnp.where(qshift[2] // (1 << bit_place) % 2 == 1, arrived, carried)
    shifted = jnp.roll(
        carried.reshape(count_exc, count_val, count_cond, width_y), -qshift[1], axis=3
    )
    shifted_rows = shifted.reshape(count_exc, -1)
    amplitude = excitons.reshape(count_exc, count_val, count_cond, width_y).astype(jnp.float32)
    val_table, cond_table = band_tables(phonon_g, band_index, count_val)
    blocks = []
    for mode_index in range(phonon_g.shape[0]):
        mixed_band = band_mix(amplitude, cond_table[mode_index], val_table[mode_index]).astype(
            jnp.bfloat16
        )
        blocks.append(
            lax.dot_general(
                shifted_rows,
                mixed_band.reshape(count_exc, -1),
                (((1,), (1,)), ((), ())),
                preferred_element_type=jnp.float32,
            )
        )
    partial_value = jnp.stack(blocks)
    norm_factor = 1.0 / math.sqrt(count_val * count_cond * width_y * planes_x * planes_z)
    own_cols = lax.psum_scatter(partial_value, ("ky", "ex"), scatter_dimension=2, tiled=True)
    coupling = lax.psum_scatter(own_cols, "kx", scatter_dimension=1, tiled=True)
    return coupling * norm_factor


def whole_step(
    planes_x, planes_z, norm_factor,
    band_hbm, q_hbm, ritz_hbm, phonon_hbm, basis_hbm, out_ref,
    band_ref, q_ref, ritz_ref, phonon_ref, basis_ref, coefs, gathered, total, exc_ref, slices, first, second_out, second_in,
    mixed, shifted, sum_out, sum_in, turned, last_out, last_in,
    load_sems, ritz_send, ritz_recv, fwd_send, fwd_recv,
    one_send, one_recv, two_send, two_recv, a_send, a_recv, b_send, b_recv,
):
    planes = planes_x * planes_z
    grp = lax.axis_index("grp")
    kx = lax.axis_index("kx")
    ky = lax.axis_index("ky")
    ex = lax.axis_index("ex")
    kz = ky * 2 + ex
    me = kx * planes_z + kz
    modes = out_ref.shape[0]
    count_exc, depth = ritz_ref.shape
    half = depth // 2
    tiles = exc_ref.shape[1] // LANES
    halves = NC // 2

    def device(plane):
        z = plane % planes_z
        return (grp, plane // planes_z, z // 2, z % 2)

    barrier = pltpu.get_barrier_semaphore()
    for step in range(1, planes):
        pl.semaphore_signal(
            barrier, inc=1, device_id=device((me + step) % planes), device_id_type=MESH
        )
    loads = [
        pltpu.make_async_copy(source, place, load_sems.at[at])
        for at, (source, place) in enumerate(
            (
                (ritz_hbm, ritz_ref),
                (band_hbm, band_ref),
                (q_hbm, q_ref),
                (phonon_hbm, phonon_ref),
                (basis_hbm, basis_ref),
            )
        )
    ]
    for load in loads:
        load.start()
    loads[0].wait()
    gathered[kx, 0] = ritz_ref[:, :half]
    gathered[kx, 1] = ritz_ref[:, half:]
    pl.semaphore_wait(barrier, planes - 1)

    asks = []
    for step in range(1, planes_x):
        ask = pltpu.make_async_remote_copy(
            src_ref=gathered.at[kx, ex],
            dst_ref=gathered.at[kx, ex],
            send_sem=ritz_send.at[step - 1],
            recv_sem=ritz_recv.at[step - 1],
            device_id=(grp, (kx + step) % planes_x, ky, ex),
            device_id_type=MESH,
        )
        ask.start()
        asks.append(ask)

    for load in loads[1:4]:
        load.wait()
    lane = lax.broadcasted_iota(jnp.int32, (modes, LANES), 1)
    low = lane < LANES // 2
    bands = [jnp.full((modes, LANES), band_ref[slot], jnp.int32) for slot in range(NV + NC)]
    part = ALLB // 2
    row_tiles = part // 2

    def rows_of(slot, base):
        found = []
        for at in range(row_tiles):
            value = None
            for band in range(base, base + part):
                start = (band * part + base // 2 + at) * LANES
                tile = phonon_ref[:, start : start + LANES].astype(jnp.float32)
                value = tile if value is None else jnp.where(bands[slot] == band, tile, value)
            found.append(value)
        return found

    def on_both(found, slot, base):
        value = found[0]
        for at in range(1, row_tiles):
            value = jnp.where((bands[slot] >> 1) == base // 2 + at, found[at], value)
        other = pltpu.roll(value, LANES // 2, 1)
        upper = (bands[slot] & 1) == jnp.where(low, 0, 1)
        return jnp.where(upper, value, other)

    for w in range(NV):
        found = rows_of(w, 0)
        for v in range(NV):
            coefs[w * NV + v, :modes, :] = on_both(found, v, 0)
    for ch in range(halves):
        lower_rows = rows_of(NV + 2 * ch, part)
        upper_rows = rows_of(NV + 2 * ch + 1, part)
        for dh in range(halves):
            for off in range(2):
                lower = on_both(lower_rows, NV + 2 * dh + off, part)
                upper = on_both(upper_rows, NV + 2 * dh + 1 - off, part)
                place = NV * NV + (ch * halves + dh) * 2 + off
                coefs[place, :modes, :] = jnp.where(low, lower, upper)
    come = lax.broadcasted_iota(jnp.int32, (LANES, LANES), 0)
    goes = lax.broadcasted_iota(jnp.int32, (LANES, LANES), 1)
    width = LANES // 2
    along = jnp.full((LANES, LANES), q_ref[1], jnp.int32)
    permute = (come == (goes & width) + ((goes + along) & (width - 1))).astype(jnp.bfloat16)
    loads[4].wait()

    def rotate(source):
        rows = jnp.concatenate([gathered[source, 0], gathered[source, 1]], axis=1)
        at = pl.multiple_of(source * depth, depth)
        return jnp.dot(
            rows, basis_ref[pl.ds(at, depth), :], preferred_element_type=jnp.float32
        )

    total[...] = rotate(kx)
    hands = []
    for step in range(1, planes_x):
        asks[step - 1].wait_recv()
        source = (kx - step + planes_x) % planes_x
        hand = pltpu.make_async_remote_copy(
            src_ref=gathered.at[source, ex],
            dst_ref=gathered.at[source, ex],
            send_sem=fwd_send.at[step - 1],
            recv_sem=fwd_recv.at[step - 1],
            device_id=(grp, kx, ky, 1 - ex),
            device_id_type=MESH,
        )
        hand.start()
        hands.append(hand)
    for step in range(1, planes_x):
        hands[step - 1].wait_recv()
        source = (kx - step + planes_x) % planes_x
        total[...] += rotate(source)
    exc_ref[...] = total[...].astype(jnp.bfloat16)

    cuts = planes // tiles
    rows_cut = count_exc // cuts
    rows_half = rows_cut // 2
    for tile in range(tiles):
        moved = jnp.dot(
            exc_ref[:, tile * LANES : (tile + 1) * LANES],
            permute,
            preferred_element_type=jnp.float32,
        ).astype(jnp.bfloat16)
        for cut in range(cuts):
            for part_of in range(2):
                at = cut * rows_cut + part_of * rows_half
                slices[cut * tiles + tile, part_of] = moved[at : at + rows_half]

    ones = []
    for step in range(1, planes):
        target = (me + step) % planes
        one = pltpu.make_async_remote_copy(
            src_ref=slices.at[target],
            dst_ref=first.at[me],
            send_sem=one_send.at[step - 1],
            recv_sem=one_recv.at[step - 1],
            device_id=device(target),
            device_id_type=MESH,
        )
        one.start()
        ones.append(one)
    first[me] = slices[me]

    own_rows = count_exc // planes_z
    chunk = 16
    per_block = own_rows // chunk

    def mix_rows(index, carry):
        at = pl.multiple_of(index * chunk, chunk)
        straight = []
        crossed = []
        for tile in range(tiles):
            part = exc_ref[pl.ds(at, chunk), tile * LANES : (tile + 1) * LANES].astype(jnp.float32)
            straight.append(part)
            crossed.append(pltpu.roll(part, LANES // 2, 1))
        block = index // per_block
        row = pl.multiple_of((index % per_block) * chunk, chunk)

        def mix_mode(u, inner):
            for v in range(NV):
                for ch in range(halves):
                    value = None
                    for dh in range(halves):
                        for off in range(2):
                            factor = coefs[NV * NV + (ch * halves + dh) * 2 + off, pl.ds(u, 1), :]
                            term = factor * (crossed if off else straight)[v * halves + dh]
                            value = term if value is None else value + term
                    minus = None
                    for w in range(NV):
                        term = coefs[w * NV + v, pl.ds(u, 1), :] * straight[w * halves + ch]
                        minus = term if minus is None else minus + term
                    tile = v * halves + ch
                    mixed[block, u, pl.ds(row, chunk), tile * LANES : (tile + 1) * LANES] = (
                        value - minus
                    ).astype(jnp.bfloat16)
            return inner

        return lax.fori_loop(0, modes, mix_mode, carry)

    lax.fori_loop(0, count_exc // chunk, mix_rows, 0)

    for one in ones:
        one.wait_recv()

    along_x = jnp.full((1, LANES), q_ref[0], jnp.int32)
    along_z = jnp.full((1, LANES), q_ref[2], jnp.int32)

    def pick(target, part_of):
        x, z = target // planes_z, target % planes_z
        value = None
        for dx in range(1, planes_x):
            for dz in range(1, planes_z):
                plane = ((x + dx) % planes_x) * planes_z + (z + dz) % planes_z
                there = first[plane, part_of]
                if value is None:
                    value = there
                else:
                    value = jnp.where((along_x == dx) & (along_z == dz), there, value)
        return value

    twos = []
    for order in range(2):
        for step in range(1, planes):
            target = (me + step) % planes
            part_of = (target // planes_z + order + 1) % 2
            second_out[target, order] = pick(target, part_of)
            at = order * (planes - 1) + step - 1
            two = pltpu.make_async_remote_copy(
                src_ref=second_out.at[target, order],
                dst_ref=second_in.at[me, order],
                send_sem=two_send.at[at],
                recv_sem=two_recv.at[at],
                device_id=device(target),
                device_id_type=MESH,
            )
            two.start()
            twos.append(two)
        second_in[me, order] = pick(me, (kx + order + 1) % 2)

    def product(order, block):
        right = mixed[block].reshape(modes * own_rows, tiles * LANES)
        return lax.dot_general(
            shifted[order], right, (((1,), (1,)), ((), ())), preferred_element_type=jnp.float32
        )

    sums = []
    mine = []
    for order in range(2):
        for two in twos[order * (planes - 1) : (order + 1) * (planes - 1)]:
            two.wait_recv()
        for cut in range(cuts):
            for tile in range(tiles):
                rows = slice(cut * rows_half, (cut + 1) * rows_half)
                lanes = slice(tile * LANES, (tile + 1) * LANES)
                shifted[order, rows, lanes] = second_in[cut * tiles + tile, order]
        for step in range(1, planes_z):
            block = (kz + step) % planes_z
            at = order * (planes_z - 1) + step - 1
            sum_out[at] = product(order, block).astype(jnp.bfloat16)
            one_sum = pltpu.make_async_remote_copy(
                src_ref=sum_out.at[at],
                dst_ref=sum_in.at[at],
                send_sem=a_send.at[at],
                recv_sem=a_recv.at[at],
                device_id=(grp, kx, block // 2, block % 2),
                device_id_type=MESH,
            )
            one_sum.start()
            sums.append(one_sum)
        mine.append(product(order, kz))
    lasts = []
    for order in range(2):
        value = mine[order]
        for at in range(order * (planes_z - 1), (order + 1) * (planes_z - 1)):
            sums[at].wait_recv()
            value = value + sum_in[at].astype(jnp.float32)
        for cut in range(cuts):
            turned[order, cut] = value[cut * rows_half : (cut + 1) * rows_half]
        for step in range(1 + order, planes_x, 2):
            block = (kx + step) % planes_x
            last_out[step - 1] = turned[order, block // 2].astype(jnp.bfloat16)
            one_last = pltpu.make_async_remote_copy(
                src_ref=last_out.at[step - 1],
                dst_ref=last_in.at[step - 1],
                send_sem=b_send.at[step - 1],
                recv_sem=b_recv.at[step - 1],
                device_id=(grp, block, ky, ex),
                device_id_type=MESH,
            )
            one_last.start()
            lasts.append((step, one_last))
    result = turned[1, kx // 2]
    for step, one_last in lasts:
        one_last.wait_recv()
        result = result + last_in[step - 1].astype(jnp.float32)
    result = result * norm_factor
    for u in range(modes):
        out_ref[u] = result[:, u * own_rows : (u + 1) * own_rows]
    for started in asks + hands + ones + twos + sums + [last for step, last in lasts]:
        started.wait_send()


def by_kernel(basis, ritz, phonon_g, band_index, qshift):
    planes_x = lax.axis_size("kx")
    planes_z = lax.axis_size(("ky", "ex"))
    planes = planes_x * planes_z
    count_basis, count_trans = basis.shape[0], basis.shape[3]
    depth, count_exc = ritz.shape
    modes = phonon_g.shape[0]
    tiles = count_trans // LANES
    rows_cut = count_exc // (planes // tiles)
    own = count_exc // planes_z
    out_rows = count_exc // planes_x
    norm_factor = 1.0 / math.sqrt(count_trans * planes)
    bf16 = jnp.bfloat16
    dma = pltpu.SemaphoreType.DMA
    vmem = pl.BlockSpec(memory_space=pltpu.VMEM)
    stay = pl.BlockSpec(memory_space=pl.ANY)
    return pl.pallas_call(
        functools.partial(whole_step, planes_x, planes_z, norm_factor),
        out_shape=jax.ShapeDtypeStruct((modes, out_rows, own), jnp.float32),
        in_specs=[stay] * 5,
        out_specs=vmem,
        scratch_shapes=[
            pltpu.SMEM(band_index.shape, jnp.int32),
            pltpu.SMEM(qshift.shape, jnp.int32),
            pltpu.VMEM((count_exc, depth), bf16),
            pltpu.VMEM((modes, phonon_g.shape[3]), bf16),
            pltpu.VMEM((count_basis, count_trans), bf16),
            pltpu.VMEM((NV * NV + NC * NC // 2, 8, LANES), jnp.float32),
            pltpu.VMEM((planes_x, 2, count_exc, depth // 2), bf16),
            pltpu.VMEM((count_exc, count_trans), jnp.float32),
            pltpu.VMEM((count_exc, count_trans), bf16),
            pltpu.VMEM((planes, 2, rows_cut // 2, LANES), bf16),
            pltpu.VMEM((planes, 2, rows_cut // 2, LANES), bf16),
            pltpu.VMEM((planes, 2, rows_cut // 2, LANES), bf16),
            pltpu.VMEM((planes, 2, rows_cut // 2, LANES), bf16),
            pltpu.VMEM((planes_z, modes, own, count_trans), bf16),
            pltpu.VMEM((2, count_exc // 2, count_trans), bf16),
            pltpu.VMEM((2 * (planes_z - 1), count_exc // 2, modes * own), bf16),
            pltpu.VMEM((2 * (planes_z - 1), count_exc // 2, modes * own), bf16),
            pltpu.VMEM((2, planes_x // 2, out_rows, modes * own), jnp.float32),
            pltpu.VMEM((planes_x - 1, out_rows, modes * own), bf16),
            pltpu.VMEM((planes_x - 1, out_rows, modes * own), bf16),
            dma((5,)),
            dma((planes_x - 1,)),
            dma((planes_x - 1,)),
            dma((planes_x - 1,)),
            dma((planes_x - 1,)),
            dma((planes - 1,)),
            dma((planes - 1,)),
            dma((2 * (planes - 1),)),
            dma((2 * (planes - 1),)),
            dma((2 * (planes_z - 1),)),
            dma((2 * (planes_z - 1),)),
            dma((planes_x - 1,)),
            dma((planes_x - 1,)),
        ],
        compiler_params=pltpu.CompilerParams(
            collective_id=0, has_side_effects=True, vmem_limit_bytes=60 << 20
        ),
    )(
        band_index,
        qshift,
        ritz.T,
        phonon_g.reshape(modes, -1),
        basis.reshape(count_basis, count_trans),
    )


def shards(basis, ritz, phonon_g, band_index, qshift):
    planes_x = lax.axis_size("kx")
    planes_z = lax.axis_size(("ky", "ex"))
    planes = planes_x * planes_z
    count_exc = ritz.shape[1]
    tiles = basis.shape[3] // LANES
    whole_tiles = (
        basis.shape[3] == NV * NC * LANES // 2
        and lax.axis_size("ex") == 2
        and planes % tiles == 0
        and planes_x * tiles == 2 * planes
        and count_exc % (planes // tiles * 32) == 0
        and count_exc % (planes_z * 16) == 0
        and count_exc % (planes_x * 16) == 0
        and ritz.shape[0] % (2 * LANES) == 0
        and phonon_g.shape[0] <= 8
    )
    step = by_kernel if whole_tiles else by_collectives
    return step(basis, ritz, phonon_g, band_index, qshift)


def solution(mesh):
    placed = (
        P(None, "kx", ("ky", "ex"), None),
        P("kx", None),
        P(None, "kx", ("ky", "ex"), None),
        P(),
        P("grp"),
    )
    return jax.shard_map(
        shards, mesh=mesh, in_specs=placed, out_specs=P("grp", "kx", ("ky", "ex")), check_vma=False
    )
```

```python
import functools
import math

import jax
import jax.numpy as jnp
from jax import lax
from jax.experimental import pallas as pl
from jax.experimental.pallas import tpu as pltpu
from jax.sharding import PartitionSpec as P

NV = 4
NC = 4
ALLB = 16
LANES = 128
MESH = pl.DeviceIdType.MESH


def passed_along(value, axis, steps):
    count = lax.axis_size(axis)
    pairs = [(source, (source + steps) % count) for source in range(count)]
    return lax.ppermute(value, axis, pairs)


def band_mix(amplitude, cond_mode, val_mode):
    cond_part = jnp.sum(cond_mode[None, None] * amplitude[:, :, None], axis=3)
    val_part = jnp.sum(val_mode[None, :, :, None] * amplitude[:, :, None], axis=1)
    return cond_part - val_part


def band_tables(phonon_g, band_index, count_val):
    all_bands = ALLB
    labels = jnp.arange(all_bands, dtype=jnp.int32)
    selector = (band_index[:, None] == labels[None, :]).astype(jnp.bfloat16)
    val_select = selector[:count_val]
    cond_select = selector[count_val:]
    coupling_table = phonon_g.reshape(phonon_g.shape[0], all_bands, all_bands, -1)
    val_table = jnp.einsum(
        "ia,uabk,jb->uijk",
        val_select,
        coupling_table,
        val_select,
        preferred_element_type=jnp.float32,
    )
    cond_table = jnp.einsum(
        "ia,uabk,jb->uijk",
        cond_select,
        coupling_table,
        cond_select,
        preferred_element_type=jnp.float32,
    )
    return (val_table, cond_table)


def by_collectives(basis, ritz, phonon_g, band_index, qshift):
    count_exc = ritz.shape[1]
    count_val = NV
    count_cond = NC
    width_y = basis.shape[3] // (count_val * count_cond)
    basis_flat = basis.reshape(basis.shape[0], -1)
    excitons = lax.dot_general(
        lax.all_gather(ritz, "kx", axis=0, tiled=True),
        basis_flat,
        (((0,), (0,)), ((), ())),
        preferred_element_type=jnp.float32,
    ).astype(jnp.bfloat16)
    planes_x = lax.axis_size("kx")
    planes_z = lax.axis_size(("ky", "ex"))
    carried = excitons
    for bit_place in range(planes_x.bit_length() - 1):
        arrived = passed_along(carried, "kx", -(1 << bit_place))
        carried = jnp.where(qshift[0] // (1 << bit_place) % 2 == 1, arrived, carried)
    for bit_place in range(planes_z.bit_length() - 1):
        arrived = passed_along(carried, ("ky", "ex"), -(1 << bit_place))
        carried = jnp.where(qshift[2] // (1 << bit_place) % 2 == 1, arrived, carried)
    shifted = jnp.roll(
        carried.reshape(count_exc, count_val, count_cond, width_y), -qshift[1], axis=3
    )
    shifted_rows = shifted.reshape(count_exc, -1)
    amplitude = excitons.reshape(count_exc, count_val, count_cond, width_y).astype(jnp.float32)
    val_table, cond_table = band_tables(phonon_g, band_index, count_val)
    blocks = []
    for mode_index in range(phonon_g.shape[0]):
        mixed_band = band_mix(amplitude, cond_table[mode_index], val_table[mode_index]).astype(
            jnp.bfloat16
        )
        blocks.append(
            lax.dot_general(
                shifted_rows,
                mixed_band.reshape(count_exc, -1),
                (((1,), (1,)), ((), ())),
                preferred_element_type=jnp.float32,
            )
        )
    partial_value = jnp.stack(blocks)
    norm_factor = 1.0 / math.sqrt(count_val * count_cond * width_y * planes_x * planes_z)
    own_cols = lax.psum_scatter(partial_value, ("ky", "ex"), scatter_dimension=2, tiled=True)
    coupling = lax.psum_scatter(own_cols, "kx", scatter_dimension=1, tiled=True)
    return coupling * norm_factor


def whole_step(
    planes_x, planes_z, norm_factor,
    band_hbm, q_hbm, ritz_hbm, phonon_hbm, basis_hbm, out_ref,
    band_ref, q_ref, ritz_ref, phonon_ref, basis_ref, coefs, gathered, total, exc_ref, slices, first, second_out, second_in, shifts,
    mixed, shifted, sum_out, sum_in, turned, last_out, last_in,
    load_sems, swap_sems, ritz_send, ritz_recv, fwd_send, fwd_recv,
    one_send, one_recv, two_send, two_recv, a_send, a_recv, b_send, b_recv,
):
    planes = planes_x * planes_z
    grp = lax.axis_index("grp")
    kx = lax.axis_index("kx")
    ky = lax.axis_index("ky")
    ex = lax.axis_index("ex")
    kz = ky * 2 + ex
    me = kx * planes_z + kz
    modes = out_ref.shape[0]
    count_exc, depth = ritz_ref.shape
    half = depth // 2
    tiles = exc_ref.shape[1] // LANES
    halves = NC // 2

    def device(plane, group):
        z = plane % planes_z
        return (group, plane // planes_z, z // 2, z % 2)

    barrier = pltpu.get_barrier_semaphore()
    for step in range(1, 2 * planes):
        pl.semaphore_signal(
            barrier,
            inc=1,
            device_id=device((me + step) % planes, (grp + step // planes) % 2),
            device_id_type=MESH,
        )
    loads = [
        pltpu.make_async_copy(source, place, load_sems.at[at])
        for at, (source, place) in enumerate(
            (
                (ritz_hbm, ritz_ref),
                (band_hbm, band_ref),
                (q_hbm, q_ref),
                (phonon_hbm, phonon_ref),
                (basis_hbm, basis_ref),
            )
        )
    ]
    for load in loads:
        load.start()
    loads[0].wait()
    gathered[kx, 0] = ritz_ref[:, :half]
    gathered[kx, 1] = ritz_ref[:, half:]
    pl.semaphore_wait(barrier, 2 * planes - 1)

    asks = []
    for step in range(1, planes_x):
        ask = pltpu.make_async_remote_copy(
            src_ref=gathered.at[kx, ex],
            dst_ref=gathered.at[kx, ex],
            send_sem=ritz_send.at[step - 1],
            recv_sem=ritz_recv.at[step - 1],
            device_id=(grp, (kx + step) % planes_x, ky, ex),
            device_id_type=MESH,
        )
        ask.start()
        asks.append(ask)

    for load in loads[1:4]:
        load.wait()
    first_row = lax.broadcasted_iota(jnp.int32, (8, LANES), 0) == 0
    along_x = jnp.full((8, LANES), q_ref[0], jnp.int32)
    along_z = jnp.full((8, LANES), q_ref[2], jnp.int32)
    shifts[grp] = jnp.where(first_row, along_x, along_z)
    swap = pltpu.make_async_remote_copy(
        src_ref=shifts.at[grp],
        dst_ref=shifts.at[grp],
        send_sem=swap_sems.at[0],
        recv_sem=swap_sems.at[1],
        device_id=(1 - grp, kx, ky, ex),
        device_id_type=MESH,
    )
    swap.start()
    lane = lax.broadcasted_iota(jnp.int32, (modes, LANES), 1)
    low = lane < LANES // 2
    bands = [jnp.full((modes, LANES), band_ref[slot], jnp.int32) for slot in range(NV + NC)]
    part = ALLB // 2
    row_tiles = part // 2

    def rows_of(slot, base):
        found = []
        for at in range(row_tiles):
            value = None
            for band in range(base, base + part):
                start = (band * part + base // 2 + at) * LANES
                tile = phonon_ref[:, start : start + LANES].astype(jnp.float32)
                value = tile if value is None else jnp.where(bands[slot] == band, tile, value)
            found.append(value)
        return found

    def on_both(found, slot, base):
        value = found[0]
        for at in range(1, row_tiles):
            value = jnp.where((bands[slot] >> 1) == base // 2 + at, found[at], value)
        other = pltpu.roll(value, LANES // 2, 1)
        upper = (bands[slot] & 1) == jnp.where(low, 0, 1)
        return jnp.where(upper, value, other)

    for w in range(NV):
        found = rows_of(w, 0)
        for v in range(NV):
            coefs[w * NV + v, :modes, :] = on_both(found, v, 0)
    for ch in range(halves):
        lower_rows = rows_of(NV + 2 * ch, part)
        upper_rows = rows_of(NV + 2 * ch + 1, part)
        for dh in range(halves):
            for off in range(2):
                lower = on_both(lower_rows, NV + 2 * dh + off, part)
                upper = on_both(upper_rows, NV + 2 * dh + 1 - off, part)
                place = NV * NV + (ch * halves + dh) * 2 + off
                coefs[place, :modes, :] = jnp.where(low, lower, upper)
    come = lax.broadcasted_iota(jnp.int32, (LANES, LANES), 0)
    goes = lax.broadcasted_iota(jnp.int32, (LANES, LANES), 1)
    width = LANES // 2
    along = jnp.full((LANES, LANES), q_ref[1], jnp.int32)
    permute = (come == (goes & width) + ((goes + along) & (width - 1))).astype(jnp.bfloat16)
    loads[4].wait()

    def rotate(source):
        rows = jnp.concatenate([gathered[source, 0], gathered[source, 1]], axis=1)
        at = pl.multiple_of(source * depth, depth)
        return jnp.dot(
            rows, basis_ref[pl.ds(at, depth), :], preferred_element_type=jnp.float32
        )

    total[...] = rotate(kx)
    hands = []
    for step in range(1, planes_x):
        asks[step - 1].wait_recv()
        source = (kx - step + planes_x) % planes_x
        hand = pltpu.make_async_remote_copy(
            src_ref=gathered.at[source, ex],
            dst_ref=gathered.at[source, ex],
            send_sem=fwd_send.at[step - 1],
            recv_sem=fwd_recv.at[step - 1],
            device_id=(grp, kx, ky, 1 - ex),
            device_id_type=MESH,
        )
        hand.start()
        hands.append(hand)
    for step in range(1, planes_x):
        hands[step - 1].wait_recv()
        source = (kx - step + planes_x) % planes_x
        total[...] += rotate(source)
    exc_ref[...] = total[...].astype(jnp.bfloat16)

    cuts = planes // tiles
    rows_cut = count_exc // cuts
    rows_half = rows_cut // 2
    for tile in range(tiles):
        moved = exc_ref[:, tile * LANES : (tile + 1) * LANES]
        for cut in range(cuts):
            for part_of in range(2):
                at = cut * rows_cut + part_of * rows_half
                slices[cut * tiles + tile, part_of] = moved[at : at + rows_half]

    ones = []
    for step in range(1, planes):
        target = (me + step) % planes
        one = pltpu.make_async_remote_copy(
            src_ref=slices.at[target, grp],
            dst_ref=first.at[me],
            send_sem=one_send.at[step - 1],
            recv_sem=one_recv.at[step - 1],
            device_id=device(target, grp),
            device_id_type=MESH,
        )
        one.start()
        ones.append(one)
    first[me] = slices[me, grp]

    own_rows = count_exc // planes_z
    chunk = 16
    per_block = own_rows // chunk

    def mix_rows(index, carry):
        at = pl.multiple_of(index * chunk, chunk)
        straight = []
        crossed = []
        for tile in range(tiles):
            part = exc_ref[pl.ds(at, chunk), tile * LANES : (tile + 1) * LANES].astype(jnp.float32)
            straight.append(part)
            crossed.append(pltpu.roll(part, LANES // 2, 1))
        block = index // per_block
        row = pl.multiple_of((index % per_block) * chunk, chunk)

        def mix_mode(u, inner):
            for v in range(NV):
                for ch in range(halves):
                    value = None
                    for dh in range(halves):
                        for off in range(2):
                            factor = coefs[NV * NV + (ch * halves + dh) * 2 + off, pl.ds(u, 1), :]
                            term = factor * (crossed if off else straight)[v * halves + dh]
                            value = term if value is None else value + term
                    minus = None
                    for w in range(NV):
                        term = coefs[w * NV + v, pl.ds(u, 1), :] * straight[w * halves + ch]
                        minus = term if minus is None else minus + term
                    tile = v * halves + ch
                    mixed[block, u, pl.ds(row, chunk), tile * LANES : (tile + 1) * LANES] = (
                        value - minus
                    ).astype(jnp.bfloat16)
            return inner

        return lax.fori_loop(0, modes, mix_mode, carry)

    chunks = count_exc // chunk
    lax.fori_loop(0, chunks // 2, mix_rows, 0)

    for one in ones:
        one.wait_recv()

    swap.wait_recv()

    def pick(x, z, group):
        row_x = shifts[group, 0:1, :]
        row_z = shifts[group, 1:2, :]
        value = None
        for dx in range(1, planes_x):
            for dz in range(1, planes_z):
                there = first[((x + dx) % planes_x) * planes_z + (z + dz) % planes_z]
                if value is None:
                    value = there
                else:
                    value = jnp.where((row_x == dx) & (row_z == dz), there, value)
        return value

    def second(dx, dz, dg):
        x, z, group = (kx + dx) % planes_x, (kz + dz) % planes_z, (grp + dg) % 2
        plane = x * planes_z + z
        at = (dg * planes_x + dx) * planes_z + dz
        return pltpu.make_async_remote_copy(
            src_ref=second_out.at[group, plane],
            dst_ref=second_in.at[grp, me],
            send_sem=two_send.at[at],
            recv_sem=two_recv.at[at],
            device_id=device(plane, group),
            device_id_type=MESH,
        )

    def send_second(dx, dz, dg):
        x, z, group = (kx + dx) % planes_x, (kz + dz) % planes_z, (grp + dg) % 2
        second_out[group, x * planes_z + z] = pick(x, z, group)
        second(dx, dz, dg).start()

    def others(parity, act):
        for far in reversed(range(planes_x // 2)):
            dx = 2 * far + parity
            for dz in range(planes_z):
                for dg in (1, 0):
                    if far == 0 and dz == 0 and dg == 0:
                        pl.when(parity != 0)(functools.partial(act, dx, dz, dg))
                    else:
                        act(dx, dz, dg)

    early = (grp + kx + 1) % 2
    others(early, send_second)
    others(1 - early, send_second)
    second_in[grp, me] = pick(kx, kz, grp)
    lax.fori_loop(chunks // 2, chunks, mix_rows, 0)

    def product(order, block):
        right = mixed[block].reshape(modes * own_rows, tiles * LANES)
        return lax.dot_general(
            shifted[order], right, (((1,), (1,)), ((), ())), preferred_element_type=jnp.float32
        )

    sums = []
    mine = []
    for order in range(2):
        half_of = (kx + order + 1) % 2
        for step in range(1, planes_x * planes_z + 1):
            dx, dz = (step // planes_z) % planes_x, step % planes_z
            dg = (grp + half_of) % 2
            if dx or dz:
                second(dx, dz, dg).wait_recv()
            else:
                pl.when(dg != 0)(lambda dg=dg: second(0, 0, dg).wait_recv())
        for tile in range(tiles):
            came = jnp.concatenate(
                [second_in[half_of, cut * tiles + tile] for cut in range(cuts)], axis=0
            )
            shifted[order, :, tile * LANES : (tile + 1) * LANES] = jnp.dot(
                came, permute, preferred_element_type=jnp.float32
            ).astype(jnp.bfloat16)
        for step in range(1, planes_z):
            block = (kz + step) % planes_z
            at = order * (planes_z - 1) + step - 1
            sum_out[at] = product(order, block).astype(jnp.bfloat16)
            one_sum = pltpu.make_async_remote_copy(
                src_ref=sum_out.at[at],
                dst_ref=sum_in.at[at],
                send_sem=a_send.at[at],
                recv_sem=a_recv.at[at],
                device_id=(grp, kx, block // 2, block % 2),
                device_id_type=MESH,
            )
            one_sum.start()
            sums.append(one_sum)
        mine.append(product(order, kz))
    lasts = []
    for order in range(2):
        value = mine[order]
        for at in range(order * (planes_z - 1), (order + 1) * (planes_z - 1)):
            sums[at].wait_recv()
            value = value + sum_in[at].astype(jnp.float32)
        for cut in range(cuts):
            turned[order, cut] = value[cut * rows_half : (cut + 1) * rows_half]
        for step in range(1 + order, planes_x, 2):
            block = (kx + step) % planes_x
            last_out[step - 1] = turned[order, block // 2].astype(jnp.bfloat16)
            one_last = pltpu.make_async_remote_copy(
                src_ref=last_out.at[step - 1],
                dst_ref=last_in.at[step - 1],
                send_sem=b_send.at[step - 1],
                recv_sem=b_recv.at[step - 1],
                device_id=(grp, block, ky, ex),
                device_id_type=MESH,
            )
            one_last.start()
            lasts.append((step, one_last))
    result = turned[1, kx // 2]
    for step, one_last in lasts:
        one_last.wait_recv()
        result = result + last_in[step - 1].astype(jnp.float32)
    result = result * norm_factor
    for u in range(modes):
        out_ref[u] = result[:, u * own_rows : (u + 1) * own_rows]
    for started in [swap] + asks + hands + ones + sums + [last for step, last in lasts]:
        started.wait_send()
    others(early, lambda *way: second(*way).wait_send())
    others(1 - early, lambda *way: second(*way).wait_send())


def by_kernel(basis, ritz, phonon_g, band_index, qshift):
    planes_x = lax.axis_size("kx")
    planes_z = lax.axis_size(("ky", "ex"))
    planes = planes_x * planes_z
    count_basis, count_trans = basis.shape[0], basis.shape[3]
    depth, count_exc = ritz.shape
    modes = phonon_g.shape[0]
    tiles = count_trans // LANES
    rows_cut = count_exc // (planes // tiles)
    own = count_exc // planes_z
    out_rows = count_exc // planes_x
    norm_factor = 1.0 / math.sqrt(count_trans * planes)
    bf16 = jnp.bfloat16
    dma = pltpu.SemaphoreType.DMA
    vmem = pl.BlockSpec(memory_space=pltpu.VMEM)
    stay = pl.BlockSpec(memory_space=pl.ANY)
    return pl.pallas_call(
        functools.partial(whole_step, planes_x, planes_z, norm_factor),
        out_shape=jax.ShapeDtypeStruct((modes, out_rows, own), jnp.float32),
        in_specs=[stay] * 5,
        out_specs=vmem,
        scratch_shapes=[
            pltpu.SMEM(band_index.shape, jnp.int32),
            pltpu.SMEM(qshift.shape, jnp.int32),
            pltpu.VMEM((count_exc, depth), bf16),
            pltpu.VMEM((modes, phonon_g.shape[3]), bf16),
            pltpu.VMEM((count_basis, count_trans), bf16),
            pltpu.VMEM((NV * NV + NC * NC // 2, 8, LANES), jnp.float32),
            pltpu.VMEM((planes_x, 2, count_exc, depth // 2), bf16),
            pltpu.VMEM((count_exc, count_trans), jnp.float32),
            pltpu.VMEM((count_exc, count_trans), bf16),
            pltpu.VMEM((planes, 2, rows_cut // 2, LANES), bf16),
            pltpu.VMEM((planes, rows_cut // 2, LANES), bf16),
            pltpu.VMEM((2, planes, rows_cut // 2, LANES), bf16),
            pltpu.VMEM((2, planes, rows_cut // 2, LANES), bf16),
            pltpu.VMEM((2, 8, LANES), jnp.int32),
            pltpu.VMEM((planes_z, modes, own, count_trans), bf16),
            pltpu.VMEM((2, count_exc // 2, count_trans), bf16),
            pltpu.VMEM((2 * (planes_z - 1), count_exc // 2, modes * own), bf16),
            pltpu.VMEM((2 * (planes_z - 1), count_exc // 2, modes * own), bf16),
            pltpu.VMEM((2, planes_x // 2, out_rows, modes * own), jnp.float32),
            pltpu.VMEM((planes_x - 1, out_rows, modes * own), bf16),
            pltpu.VMEM((planes_x - 1, out_rows, modes * own), bf16),
            dma((5,)),
            dma((2,)),
            dma((planes_x - 1,)),
            dma((planes_x - 1,)),
            dma((planes_x - 1,)),
            dma((planes_x - 1,)),
            dma((planes - 1,)),
            dma((planes - 1,)),
            dma((2 * planes,)),
            dma((2 * planes,)),
            dma((2 * (planes_z - 1),)),
            dma((2 * (planes_z - 1),)),
            dma((planes_x - 1,)),
            dma((planes_x - 1,)),
        ],
        compiler_params=pltpu.CompilerParams(
            collective_id=0, has_side_effects=True, vmem_limit_bytes=60 << 20
        ),
    )(
        band_index,
        qshift,
        ritz.T,
        phonon_g.reshape(modes, -1),
        basis.reshape(count_basis, count_trans),
    )


def shards(basis, ritz, phonon_g, band_index, qshift):
    planes_x = lax.axis_size("kx")
    planes_z = lax.axis_size(("ky", "ex"))
    planes = planes_x * planes_z
    count_exc = ritz.shape[1]
    tiles = basis.shape[3] // LANES
    whole_tiles = (
        basis.shape[3] == NV * NC * LANES // 2
        and lax.axis_size("ex") == 2
        and lax.axis_size("grp") == 2
        and planes % tiles == 0
        and planes_x * tiles == 2 * planes
        and count_exc % (planes // tiles * 32) == 0
        and count_exc % (planes_z * 16) == 0
        and count_exc % (planes_x * 16) == 0
        and ritz.shape[0] % (2 * LANES) == 0
        and phonon_g.shape[0] <= 8
    )
    step = by_kernel if whole_tiles else by_collectives
    return step(basis, ritz, phonon_g, band_index, qshift)


def solution(mesh):
    placed = (
        P(None, "kx", ("ky", "ex"), None),
        P("kx", None),
        P(None, "kx", ("ky", "ex"), None),
        P(),
        P("grp"),
    )
    return jax.shard_map(
        shards, mesh=mesh, in_specs=placed, out_specs=P("grp", "kx", ("ky", "ex")), check_vma=False
    )
```
